32 devices in a mesh: dp: 8 (over y, x, core), fsdp: 4 (over z).
Axes of the slice: x: 2, y: 2, z: 4, core: 2. Of those that a mesh axis runs over, the one named last changes fastest.
Arguments:
- layer_input: bfloat16 [2, 8, 1024, 1152], P(None, 'dp', 'fsdp'), may hold values from -6 to 6
- output_gradient: bfloat16 [2, 8, 1024, 1152], P(None, 'dp', 'fsdp'), may hold values from -6 to 6
- prefix_length: int32 [2, 8], P(None, 'dp'), may hold values from 0 to 1024
- attention_gain: bfloat16 [1152], P(('dp', 'fsdp')), may hold values from 0.5 to 1.5
- inward: bfloat16 [1152, 1536], P(('dp', 'fsdp')), may hold values from -0.1875 to 0.1875
- inward_down: bfloat16 [1152, 256], P(('dp', 'fsdp')), may hold values from -0.1875 to 0.1875
- inward_up: bfloat16 [256, 1536], P(('dp', 'fsdp')), may hold values from -0.1875 to 0.1875
- outward: bfloat16 [1024, 1152], P(('dp', 'fsdp')), may hold values from -1.5 to 1.5
- outward_down: bfloat16 [1024, 256], P(('dp', 'fsdp')), may hold values from -1.5 to 1.5
- outward_up: bfloat16 [256, 1152], P(('dp', 'fsdp')), may hold values from -0.1875 to 0.1875
- feedforward_gain: bfloat16 [1152], P(('dp', 'fsdp')), may hold values from 0.5 to 1.5
- widening: bfloat16 [1152, 13824], P(('dp', 'fsdp')), may hold values from -0.1875 to 0.1875
- widening_down: bfloat16 [1152, 256], P(('dp', 'fsdp')), may hold values from -0.1875 to 0.1875
- widening_up: bfloat16 [256, 13824], P(('dp', 'fsdp')), may hold values from -0.1875 to 0.1875
- narrowing: bfloat16 [6912, 1152], P(('dp', 'fsdp')), may hold values from -0.078125 to 0.078125
- narrowing_down: bfloat16 [6912, 256], P(('dp', 'fsdp')), may hold values from -0.078125 to 0.078125
- narrowing_up: bfloat16 [256, 1152], P(('dp', 'fsdp')), may hold values from -0.1875 to 0.1875
Outputs:
- layer_output: bfloat16 [2, 8, 1024, 1152], P(None, 'dp', 'fsdp')
- input_gradient: float32 [2, 8, 1024, 1152], P(None, 'dp', 'fsdp')
- attention_gain_gradient: float32 [1152], P(('dp', 'fsdp'))
- inward_gradient: float32 [1152, 1536], P(('dp', 'fsdp'))
- inward_down_gradient: float32 [1152, 256], P(('dp', 'fsdp'))
- inward_up_gradient: float32 [256, 1536], P(('dp', 'fsdp'))
- outward_gradient: float32 [1024, 1152], P(('dp', 'fsdp'))
- outward_down_gradient: float32 [1024, 256], P(('dp', 'fsdp'))
- outward_up_gradient: float32 [256, 1152], P(('dp', 'fsdp'))
- feedforward_gain_gradient: float32 [1152], P(('dp', 'fsdp'))
- widening_gradient: float32 [1152, 13824], P(('dp', 'fsdp'))
- widening_down_gradient: float32 [1152, 256], P(('dp', 'fsdp'))
- widening_up_gradient: float32 [256, 13824], P(('dp', 'fsdp'))
- narrowing_gradient: float32 [6912, 1152], P(('dp', 'fsdp'))
- narrowing_down_gradient: float32 [6912, 256], P(('dp', 'fsdp'))
- narrowing_up_gradient: float32 [256, 1152], P(('dp', 'fsdp'))
The draws below stay inside these ranges and needn't reach their ends.
All inputs are finite; a program needn't handle non-finite values.
Results may differ from the reference program's by a relative error of at most 0.019.
Values may be sent and summed in bfloat16 or wider, within the bound.
A program may use at most 448 MiB of HBM per device.

```python
import jax
import jax.numpy as jnp
from jax import lax

D = 1152
FF = 6912
HEADS = 4
HDIM = 256
RANK = 256
MICRO = 2
QKV = 1536
HQD = 1024
SEQS = 8
SEQ = 1024


def touch_ends(drawn, key, smallest, largest):
    extent = drawn.shape
    place = [jax.random.randint(jax.random.fold_in(key, axis), (), 0, extent[axis]) for axis in range(len(extent))]
    drawn = drawn.at[tuple(place)].set(smallest)
    longest = extent.index(max(extent))
    place[longest] = (place[longest] + 1) % extent[longest]
    return drawn.at[tuple(place)].set(largest)


def steps_of(rng, shape, cuts, smallest, largest):
    def one(position, shards_of):
        heights = jax.random.uniform(jax.random.fold_in(jax.random.fold_in(rng, 6), position), (shards_of,), jnp.float32, smallest / len(cuts), largest / len(cuts))
        return jnp.repeat(jnp.exp(heights), shape[position] // shards_of).reshape((-1,) + (1,) * (len(shape) - position - 1))

    loudness = one(*cuts[0])
    for cut in cuts[1:]:
        loudness = loudness * one(*cut)
    return loudness


def gaussian(key, extent, scale, most, split=(), kind=jnp.bfloat16):
    loudness = steps_of(key, extent, split, -0.22, 0.18) if split else 1.0
    entries = jax.random.normal(key, extent, jnp.float32) * scale * loudness
    return jnp.minimum(jnp.maximum(entries, -most), most).astype(kind)


def setup_inputs(seed: int = 0) -> dict:
    seeds = jax.random.split(jax.random.key(seed), 18)
    return {
        "layer_input": gaussian(seeds[0], (MICRO, SEQS, SEQ, D), 1.0, 6.0, ((1, 8), (2, 4))),
        "output_gradient": gaussian(seeds[1], (MICRO, SEQS, SEQ, D), 1.0, 6.0, ((1, 8), (2, 4))),
        "prefix_length": touch_ends(jax.random.randint(seeds[2], (MICRO, SEQS), 0, SEQ + 1), jax.random.fold_in(seeds[2], 1), 0, SEQ).astype(jnp.int32),
        "attention_gain": jnp.clip(1.0 + 0.1 * jax.random.normal(seeds[3], (D,), jnp.float32), 0.5, 1.5).astype(jnp.bfloat16),
        "inward": gaussian(seeds[4], (D, QKV), D ** -0.5, 0.1875, ((0, 32),)),
        "inward_down": gaussian(seeds[5], (D, RANK), D ** -0.5, 0.1875, ((0, 32),)),
        "inward_up": gaussian(seeds[6], (RANK, QKV), (4 * RANK) ** -0.5, 0.1875, ((0, 32),)),
        "outward": gaussian(seeds[7], (HQD, D), (HQD // 64) ** -0.5, 1.5, ((0, 32),)),
        "outward_down": gaussian(seeds[8], (HQD, RANK), (HQD // 64) ** -0.5, 1.5, ((0, 32),)),
        "outward_up": gaussian(seeds[9], (RANK, D), (4 * RANK) ** -0.5, 0.1875, ((0, 32),)),
        "feedforward_gain": jnp.clip(1.0 + 0.1 * jax.random.normal(seeds[10], (D,), jnp.float32), 0.5, 1.5).astype(jnp.bfloat16),
        "widening": gaussian(seeds[11], (D, 2 * FF), D ** -0.5, 0.1875, ((0, 32),)),
        "widening_down": gaussian(seeds[12], (D, RANK), D ** -0.5, 0.1875, ((0, 32),)),
        "widening_up": gaussian(seeds[13], (RANK, 2 * FF), (4 * RANK) ** -0.5, 0.1875, ((0, 32),)),
        "narrowing": gaussian(seeds[14], (FF, D), FF ** -0.5, 0.078125, ((0, 32),)),
        "narrowing_down": gaussian(seeds[15], (FF, RANK), FF ** -0.5, 0.078125, ((0, 32),)),
        "narrowing_up": gaussian(seeds[16], (RANK, D), (4 * RANK) ** -0.5, 0.1875, ((0, 32),)),
    }


@jax.custom_vjp
def low(v):
    return lax.optimization_barrier(v.astype(jnp.bfloat16)).astype(jnp.float32)

@jax.custom_vjp
def low_back(v):
    return v

def low_keep(v):
    return (low(v), None)

def low_pass(kept, grad):
    return (grad,)

def back_keep(v):
    return (v, None)

def back_low(kept, grad):
    return (low(grad),)
low.defvjp(low_keep, low_pass)
low_back.defvjp(back_keep, back_low)
EPSILON = 1e-06
THETA = 10000.0
HIGH = lax.Precision.HIGHEST

def product(left, right):
    return jnp.dot(left, right, precision=HIGH)

def rms_scale(row_block, gain):
    factor = lax.rsqrt(lax.optimization_barrier(jnp.mean(row_block * row_block, axis=-1, keepdims=True)) + EPSILON)
    return row_block * factor * gain

def adapted(row_block, base, reducer, expander):
    inner_rows = low(low_back(product(row_block, reducer)))
    return product(row_block, base) + product(inner_rows, expander)

def rotation(positions, width):
    halfway = width // 2
    frequency = jnp.power(THETA, -2.0 * jnp.arange(halfway, dtype=jnp.float32) / width)
    angles = positions.astype(jnp.float32)[:, None] * frequency[None, :]
    return (jnp.cos(angles), jnp.sin(angles))

def rotate(values, cosine, sine_part):
    halfway = values.shape[-1] // 2
    leading = values[..., :halfway]
    second = values[..., halfway:]
    return jnp.concatenate([leading * cosine - second * sine_part, second * cosine + leading * sine_part], axis=-1)

def attend(queries, keys, values, limit):
    seq_len = keys.shape[0]
    block = min(512, seq_len)
    key_pos = jnp.arange(seq_len, dtype=jnp.int32)
    scale = HDIM ** (-0.5)

    def one_block(inputs):
        query_block, start = inputs
        query_pos = start + jnp.arange(block, dtype=jnp.int32)
        scores = low_back(jnp.einsum('rhd,kd->hrk', query_block, keys, precision=HIGH) * scale)
        visible = (key_pos[None, :] <= query_pos[:, None]) | (key_pos[None, :] < limit)
        scores = jnp.where(visible[None], scores, -1e+30)
        peak = lax.optimization_barrier(jnp.max(scores, axis=-1, keepdims=True))
        powers = jnp.exp(scores - peak)
        probs = powers / lax.optimization_barrier(jnp.sum(powers, axis=-1, keepdims=True))
        return jnp.einsum('hrk,kd->rhd', low(probs), values, precision=HIGH)
    blocks = queries.reshape(seq_len // block, block, HEADS, HDIM)
    starts = jnp.arange(seq_len // block, dtype=jnp.int32) * block
    mixed = lax.map(jax.checkpoint(one_block), (blocks, starts))
    return mixed.reshape(seq_len, HEADS * HDIM)

def layer(row_block, params, limit):
    first_gain, inward, inward_down, inward_up, outward, outward_down, outward_up, second_gain, widening, widening_down, widening_up, narrowing, narrowing_down, narrowing_up = params
    seq_len = row_block.shape[0]
    query_width = HEADS * HDIM
    cosine, sine_part = rotation(jnp.arange(seq_len, dtype=jnp.int32), HDIM)
    normed_first = low(rms_scale(row_block, first_gain))
    joint = low_back(adapted(normed_first, inward, inward_down, inward_up))
    queries = low(rotate(joint[:, :query_width].reshape(seq_len, HEADS, HDIM), cosine[:, None, :], sine_part[:, None, :]))
    keys = low(rotate(joint[:, query_width:query_width + HDIM], cosine, sine_part))
    values = low(joint[:, query_width + HDIM:])
    mixed = low(low_back(attend(queries, keys, values, limit)))
    middle = row_block + low_back(adapted(mixed, outward, outward_down, outward_up))
    normed_second = low(rms_scale(middle, second_gain))
    spread = low_back(adapted(normed_second, widening, widening_down, widening_up))
    activated = low(jax.nn.gelu(spread[:, :FF], approximate=True) * spread[:, FF:])
    return middle + low_back(adapted(activated, narrowing, narrowing_down, narrowing_up))

def reference(layer_input, output_gradient, prefix_length, attention_gain, inward, inward_down, inward_up, outward, outward_down, outward_up, feedforward_gain, widening, widening_down, widening_up, narrowing, narrowing_down, narrowing_up):
    params = tuple((weight.astype(jnp.float32) for weight in (attention_gain, inward, inward_down, inward_up, outward, outward_down, outward_up, feedforward_gain, widening, widening_down, widening_up, narrowing, narrowing_down, narrowing_up)))
    seq_count = layer_input.shape[0] * layer_input.shape[1]
    rows_all = layer_input.reshape(seq_count, SEQ, D).astype(jnp.float32)
    cotangents = output_gradient.reshape(seq_count, SEQ, D).astype(jnp.float32)
    limits = prefix_length.reshape(seq_count).astype(jnp.int32)
    zeros = tuple((jnp.zeros_like(weight) for weight in params))

    def visit(totals, item):
        row_block, cotangent, limit = item

        def forward(rows_in, params_in):
            return layer(rows_in, params_in, limit)
        result, pullback = jax.vjp(forward, row_block, params)
        row_grad, param_grads = pullback(cotangent)
        totals = tuple((total + grad_part for total, grad_part in zip(totals, param_grads)))
        return (totals, (result.astype(jnp.bfloat16), row_grad))
    totals, (results, row_grads) = lax.scan(visit, zeros, (rows_all, cotangents, limits))
    gain_one, inward_grad, inward_down_grad, inward_up_grad, outward_grad, outward_down_grad, outward_up_grad, gain_two, widening_grad, widening_down_grad, widening_up_grad, narrowing_grad, narrowing_down_grad, narrowing_up_grad = totals
    return (results.reshape(layer_input.shape), row_grads.reshape(layer_input.shape), gain_one, inward_grad, inward_down_grad, inward_up_grad, outward_grad, outward_down_grad, outward_up_grad, gain_two, widening_grad, widening_down_grad, widening_up_grad, narrowing_grad, narrowing_down_grad, narrowing_up_grad)
```

```python
import jax
import jax.numpy as jnp
from jax import lax
from jax.sharding import PartitionSpec as P

EPSILON = 1e-06
THETA = 10000.0
LANES = 128
HDIM = 256
BOTH = ("dp", "fsdp")
BF16 = jnp.bfloat16
F32 = jnp.float32


def product(left, right):
    return jnp.dot(left, right, preferred_element_type=F32)


def contract_rows(left, right):
    return lax.dot_general(left, right, (((0,), (0,)), ((), ())), preferred_element_type=F32)


def against(left, right):
    return lax.dot_general(left, right, (((1,), (1,)), ((), ())), preferred_element_type=F32)


def rotation(positions, width):
    halfway = width // 2
    frequency = jnp.power(THETA, -2.0 * jnp.arange(halfway, dtype=F32) / width)
    angles = positions.astype(F32)[:, None] * frequency[None, :]
    return (jnp.cos(angles), jnp.sin(angles))


def rotate(values, cosine, sine_part):
    halfway = values.shape[-1] // 2
    leading = values[..., :halfway]
    second = values[..., halfway:]
    return jnp.concatenate(
        [leading * cosine - second * sine_part, second * cosine + leading * sine_part], axis=-1
    )


def gelu_parts(v):
    inner = 0.7978845608028654 * (v + 0.044715 * v * v * v)
    t = jnp.tanh(inner)
    value = 0.5 * v * (1.0 + t)
    slope = 0.5 * (1.0 + t) + 0.5 * v * (1.0 - t * t) * (
        0.7978845608028654 * (1.0 + 3.0 * 0.044715 * v * v)
    )
    return value, slope


def gather_packed(pieces, count):
    flat = [piece.reshape(-1, LANES) for piece in pieces]
    sizes = [f.shape[0] for f in flat]
    packed = jnp.concatenate(flat, axis=0)
    spare = -packed.shape[0] % 8
    packed = jnp.pad(packed, ((0, spare), (0, 0)))
    full = lax.all_gather(packed, BOTH, axis=0, tiled=False)
    out, at = [], 0
    for piece, size in zip(pieces, sizes):
        part = full[:, at : at + size]
        out.append(part.reshape(count * piece.shape[0], piece.shape[1]))
        at += size
    return out


def scatter_packed(grads, count):
    flat = [g.astype(BF16).reshape(count, -1, LANES) for g in grads]
    sizes = [f.shape[1] for f in flat]
    packed = jnp.concatenate(flat, axis=1)
    spare = -packed.shape[1] % 64
    packed = jnp.pad(packed, ((0, 0), (0, spare), (0, 0)))
    rows = packed.shape[1]
    summed = lax.psum_scatter(
        packed.reshape(count * rows, LANES), BOTH, scatter_dimension=0, tiled=True
    )
    out, at = [], 0
    for g, size in zip(grads, sizes):
        out.append(summed[at : at + size].reshape(g.shape[0] // count, g.shape[1]).astype(F32))
        at += size
    return out


def per_device_of(ND, NF):
    COUNT = ND * NF

    def per_device(
        layer_input,
        output_gradient,
        prefix_length,
        attention_gain,
        inward,
        inward_down,
        inward_up,
        outward,
        outward_down,
        outward_up,
        feedforward_gain,
        widening,
        widening_down,
        widening_up,
        narrowing,
        narrowing_down,
        narrowing_up,
    ):
        micro_count, _, T, D = layer_input.shape
        QKV = inward.shape[1]
        query_width = outward.shape[0] * COUNT
        HEADS = query_width // HDIM
        FF = widening.shape[1] // 2
        RANK = widening_down.shape[1]
        FS = FF // ND
        FP = -(-FS // LANES) * LANES
        ROWS = D // COUNT
        UPS = RANK // COUNT
        scale = HDIM ** (-0.5)

        gains = jnp.pad(
            jnp.stack([attention_gain, feedforward_gain]), ((0, 0), (0, LANES - ROWS))
        )
        gains_full, inward_full, inward_down_full, inward_up_full = gather_packed(
            (gains, inward, inward_down, inward_up), COUNT
        )
        gains_full = gains_full.reshape(COUNT, 2, LANES)[:, :, :ROWS].astype(F32)
        first_gain = gains_full[:, 0].reshape(D)
        second_gain = gains_full[:, 1].reshape(D)
        (
            outward_full,
            outward_down_full,
            outward_up_full,
            widening_down_full,
            narrowing_up_full,
        ) = gather_packed((outward, outward_down, outward_up, widening_down, narrowing_up), COUNT)

        wide = jnp.concatenate([widening, widening_up], axis=0)
        wide = wide.reshape(ROWS + UPS, 2, ND, FS)
        wide = jnp.pad(wide, ((0, 0), (0, 0), (0, 0), (0, FP - FS)))
        wide = wide.transpose(2, 0, 1, 3).reshape(ND, ROWS + UPS, 2 * FP)
        wide = lax.all_to_all(wide, "dp", 0, 0, tiled=True)
        wide = lax.all_gather(wide, "fsdp", axis=0, tiled=False)
        wide = wide.transpose(1, 0, 2, 3)
        widening_slice = wide[:, :, :ROWS].reshape(D, 2 * FP)
        widening_up_slice = wide[:, :, ROWS:].reshape(RANK, 2 * FP)
        narrow = jnp.concatenate([narrowing, narrowing_down], axis=1)
        narrow = lax.all_gather(narrow, "fsdp", axis=0, tiled=True)
        narrow = jnp.pad(narrow, ((0, FP - FS), (0, 0)))
        narrowing_slice, narrowing_down_slice = narrow[:, :D], narrow[:, D:]

        inward_eff = (inward_full + product(inward_down_full, inward_up_full)).astype(BF16)
        outward_eff = (outward_full + product(outward_down_full, outward_up_full)).astype(BF16)
        wide_eff = (widening_slice + product(widening_down_full, widening_up_slice)).astype(BF16)
        narrow_eff = (narrowing_slice + product(narrowing_down_slice, narrowing_up_full)).astype(
            BF16
        )

        positions = lax.axis_index("fsdp") * T + jnp.arange(T, dtype=jnp.int32)
        cosine, sine_part = rotation(positions, HDIM)
        head_cosine = cosine[:, None, :]
        head_sine = sine_part[:, None, :]

        def unit(v):
            return v * lax.rsqrt(jnp.mean(v * v, axis=-1, keepdims=True) + EPSILON)

        def unit_back(v, gain, upstream):
            r = lax.rsqrt(jnp.mean(v * v, axis=-1, keepdims=True) + EPSILON)
            n = v * r
            e = upstream * gain
            back = r * (e - n * jnp.mean(e * n, axis=-1, keepdims=True))
            return back, jnp.sum(upstream * n, axis=0)

        micro = range(micro_count)
        residual = [layer_input[m, 0].astype(F32) for m in micro]
        upstream = [output_gradient[m, 0] for m in micro]
        upstream_all = [lax.all_gather(g, "dp", axis=0, tiled=True) for g in upstream]

        normed_first, queries, all_keys, all_values = [], [], [], []
        visible, logsum, mixed, middle, normed_second = [], [], [], [], []
        second_all = []

        def masked_scores(m):
            raw = (
                jnp.einsum("rhd,kd->hrk", queries[m], all_keys[m], preferred_element_type=F32)
                * scale
            )
            return jnp.where(visible[m][None], raw, -1e30)

        for m in micro:
            h1 = (unit(residual[m]) * first_gain).astype(BF16)
            normed_first.append(h1)
            joint = product(h1, inward_eff)
            queries.append(
                rotate(
                    joint[:, :query_width].reshape(T, HEADS, HDIM), head_cosine, head_sine
                ).astype(BF16)
            )
            own_keys = rotate(joint[:, query_width : query_width + HDIM], cosine, sine_part)
            own = jnp.concatenate([own_keys, joint[:, query_width + HDIM :]], axis=1).astype(BF16)
            both = lax.all_gather(own, "fsdp", axis=0, tiled=True)
            all_keys.append(both[:, :HDIM])
            all_values.append(both[:, HDIM:])
            key_pos = jnp.arange(NF * T, dtype=jnp.int32)
            limit = prefix_length[m, 0]
            visible.append(
                (key_pos[None, :] <= positions[:, None]) | (key_pos[None, :] < limit)
            )
            scores = masked_scores(m)
            peak = jnp.max(scores, axis=-1, keepdims=True)
            total = jnp.sum(jnp.exp(scores - peak), axis=-1, keepdims=True)
            logsum.append(peak + jnp.log(total))
            probs_low = jnp.exp(scores - logsum[m]).astype(BF16)
            mix = jnp.einsum("hrk,kd->rhd", probs_low, all_values[m], preferred_element_type=F32)
            mixed.append(mix.reshape(T, query_width).astype(BF16))
            middle.append(residual[m] + product(mixed[m], outward_eff))
            normed_second.append((unit(middle[m]) * second_gain).astype(BF16))
            second_all.append(lax.all_gather(normed_second[m], "dp", axis=0, tiled=True))

        outputs, middle_grad = [], []
        wide_grad = narrow_grad = None
        second_gain_grad = 0.0
        for m in micro:
            spread = product(second_all[m], wide_eff)
            gate, upper = spread[:, :FP], spread[:, FP:]
            value, slope = gelu_parts(gate)
            activated = (value * upper).astype(BF16)
            shrink = product(activated, narrow_eff).astype(BF16)
            shrink = lax.psum_scatter(shrink, "dp", scatter_dimension=0, tiled=True)
            outputs.append((middle[m] + shrink.astype(F32)).astype(BF16))
            act_grad = against(upstream_all[m], narrow_eff)
            spread_grad = jnp.concatenate(
                [act_grad * upper * slope, act_grad * value], axis=1
            ).astype(BF16)
            rows_grad = against(spread_grad, wide_eff).astype(BF16)
            rows_grad = lax.psum_scatter(rows_grad, "dp", scatter_dimension=0, tiled=True)
            part = contract_rows(activated, upstream_all[m])
            narrow_grad = part if narrow_grad is None else narrow_grad + part
            part = contract_rows(second_all[m], spread_grad)
            wide_grad = part if wide_grad is None else wide_grad + part
            back, gain_grad = unit_back(middle[m], second_gain, rows_grad.astype(F32))
            second_gain_grad = second_gain_grad + gain_grad
            middle_grad.append(upstream[m].astype(F32) + back)

        wide_grad = wide_grad.astype(BF16)
        narrow_grad = narrow_grad.astype(BF16)
        wide_up_grad = contract_rows(widening_down_full, wide_grad).astype(BF16)
        widening_down_part = against(wide_grad, widening_up_slice)
        narrowing_up_part = contract_rows(narrowing_down_slice, narrow_grad)
        wide_both = jnp.concatenate(
            [
                wide_grad.reshape(ND, NF, ROWS, 2 * FP),
                wide_up_grad.reshape(ND, NF, UPS, 2 * FP),
            ],
            axis=2,
        ).transpose(1, 0, 2, 3)
        wide_both = wide_both.reshape(NF * ND * (ROWS + UPS), 2 * FP)
        wide_both = lax.psum_scatter(wide_both, "fsdp", scatter_dimension=0, tiled=True)
        wide_both = wide_both.reshape(ND, ROWS + UPS, 2 * FP)
        wide_both = lax.all_to_all(wide_both, "dp", 0, 0, tiled=True)
        wide_both = wide_both.reshape(ND, ROWS + UPS, 2, FP)[..., :FS].transpose(1, 2, 0, 3)
        wide_both = wide_both.reshape(ROWS + UPS, 2 * FF).astype(F32)
        widening_grad, widening_up_grad = wide_both[:ROWS], wide_both[ROWS:]
        narrow_sum = lax.psum_scatter(
            narrow_grad[:FS], "fsdp", scatter_dimension=0, tiled=True
        )
        narrowing_grad = narrow_sum.astype(F32)
        narrowing_down_grad = against(narrow_sum, narrowing_up_full)

        branch_grad, joint_grads, mixed_grads = [], [], []
        for m in micro:
            branch_grad.append(middle_grad[m].astype(BF16))
        outward_part = contract_rows(
            jnp.concatenate(mixed, axis=0), jnp.concatenate(branch_grad, axis=0)
        ).astype(BF16)
        outward_up_part = contract_rows(outward_down_full, outward_part)
        (
            outward_grad,
            outward_up_grad,
            widening_down_grad,
            narrowing_up_grad,
        ) = scatter_packed(
            (outward_part, outward_up_part, widening_down_part, narrowing_up_part), COUNT
        )
        outward_down_grad = against(outward_grad.astype(BF16), outward_up_full)

        input_grads = []
        first_gain_grad = 0.0
        for m in micro:
            mixed_grad = against(branch_grad[m], outward_eff).astype(BF16)
            mixed_grad = mixed_grad.reshape(T, HEADS, HDIM)
            probs_again = jnp.exp(masked_scores(m) - logsum[m])
            prob_grad = jnp.einsum(
                "rhd,kd->hrk", mixed_grad, all_values[m], preferred_element_type=F32
            )
            center = jnp.sum(probs_again * prob_grad, axis=-1, keepdims=True)
            score_grad = (probs_again * (prob_grad - center)).astype(BF16)
            query_grad = (
                jnp.einsum("hrk,kd->rhd", score_grad, all_keys[m], preferred_element_type=F32)
                * scale
            )
            key_grad = (
                jnp.einsum("hrk,rhd->kd", score_grad, queries[m], preferred_element_type=F32)
                * scale
            )
            value_grad = jnp.einsum(
                "hrk,rhd->kd", probs_again.astype(BF16), mixed_grad, preferred_element_type=F32
            )
            both = jnp.concatenate([key_grad, value_grad], axis=1).astype(BF16)
            both = lax.psum_scatter(both, "fsdp", scatter_dimension=0, tiled=True).astype(F32)
            joint_grads.append(
                jnp.concatenate(
                    [
                        rotate(query_grad, head_cosine, -head_sine).reshape(T, query_width),
                        rotate(both[:, :HDIM], cosine, -sine_part),
                        both[:, HDIM:],
                    ],
                    axis=1,
                ).astype(BF16)
            )
            first_rows_grad = against(joint_grads[m], inward_eff)
            back, gain_grad = unit_back(residual[m], first_gain, first_rows_grad)
            first_gain_grad = first_gain_grad + gain_grad
            input_grads.append(middle_grad[m] + back)

        inward_part = contract_rows(
            jnp.concatenate(normed_first, axis=0), jnp.concatenate(joint_grads, axis=0)
        ).astype(BF16)
        inward_up_part = contract_rows(inward_down_full, inward_part)
        gain_parts = jnp.stack([first_gain_grad, second_gain_grad]).reshape(2, COUNT, ROWS)
        gain_parts = jnp.pad(gain_parts, ((0, 0), (0, 0), (0, LANES - ROWS)))
        gain_parts = gain_parts.transpose(1, 0, 2).reshape(COUNT * 2, LANES)
        inward_grad, inward_up_grad, gain_grads = scatter_packed(
            (inward_part, inward_up_part, gain_parts), COUNT
        )
        inward_down_grad = against(inward_grad.astype(BF16), inward_up_full)

        return (
            jnp.stack(outputs)[:, None],
            jnp.stack(input_grads)[:, None],
            gain_grads[0, :ROWS],
            inward_grad,
            inward_down_grad,
            inward_up_grad,
            outward_grad,
            outward_down_grad,
            outward_up_grad,
            gain_grads[1, :ROWS],
            widening_grad,
            widening_down_grad,
            widening_up_grad,
            narrowing_grad,
            narrowing_down_grad,
            narrowing_up_grad,
        )

    return per_device


def solution(mesh):
    rows = P(BOTH, None)
    tokens = P(None, "dp", "fsdp", None)
    weights = (P(BOTH),) + (rows,) * 6 + (P(BOTH),) + (rows,) * 6
    return jax.shard_map(
        per_device_of(mesh.shape["dp"], mesh.shape["fsdp"]),
        mesh=mesh,
        in_specs=(tokens, tokens, P(None, "dp")) + weights,
        out_specs=(tokens, tokens) + weights,
        check_vma=False,
    )
```

```python
import functools

import jax
import jax.numpy as jnp
from jax import lax
from jax.experimental import pallas as pl
from jax.experimental.pallas import tpu as pltpu
from jax.sharding import PartitionSpec as P

EPSILON = 1e-06
THETA = 10000.0
LANES = 128
HDIM = 256
BOTH = ("dp", "fsdp")
BF16 = jnp.bfloat16
F32 = jnp.float32


def product(left, right):
    return jnp.dot(left, right, preferred_element_type=F32)


def contract_rows(left, right):
    return lax.dot_general(left, right, (((0,), (0,)), ((), ())), preferred_element_type=F32)


def against(left, right):
    return lax.dot_general(left, right, (((1,), (1,)), ((), ())), preferred_element_type=F32)


def rotation(positions, width):
    halfway = width // 2
    frequency = jnp.power(THETA, -2.0 * jnp.arange(halfway, dtype=F32) / width)
    angles = positions.astype(F32)[:, None] * frequency[None, :]
    return (jnp.cos(angles), jnp.sin(angles))


def rotate(values, cosine, sine_part):
    halfway = values.shape[-1] // 2
    leading = values[..., :halfway]
    second = values[..., halfway:]
    return jnp.concatenate(
        [leading * cosine - second * sine_part, second * cosine + leading * sine_part], axis=-1
    )


def gelu_parts(v):
    inner = 0.7978845608028654 * (v + 0.044715 * v * v * v)
    t = jnp.tanh(inner)
    value = 0.5 * v * (1.0 + t)
    slope = 0.5 * (1.0 + t) + 0.5 * v * (1.0 - t * t) * (
        0.7978845608028654 * (1.0 + 3.0 * 0.044715 * v * v)
    )
    return value, slope


MESH = pl.DeviceIdType.MESH


def places():
    dp = lax.axis_index("dp")
    z = lax.axis_index("fsdp")
    y, x, c = dp // 4, (dp // 2) % 2, dp % 2
    at = lambda yy, xx, cc: (yy * 4 + xx * 2 + cc, z)
    return y, x, c, z, at(y, 1 - x, c), at(1 - y, x, c), at(y, x, 1 - c), dp


def hello(peer):
    pl.semaphore_signal(pltpu.get_barrier_semaphore(), inc=1, device_id=peer, device_id_type=MESH)


def greet(lines, planes, z, dp, plane_peers):
    barrier = pltpu.get_barrier_semaphore()
    base = 0
    if planes:
        base = len(plane_peers)
        for peer in plane_peers:
            hello(peer)
    if not lines:
        pl.semaphore_wait(barrier, base)
        return
    pl.when(z > 0)(lambda: hello((dp, z - 1)))
    pl.when(z < 3)(lambda: hello((dp, z + 1)))
    inner = (z > 0) & (z < 3)
    pl.when(inner)(lambda: pl.semaphore_wait(barrier, base + 2))
    pl.when(jnp.logical_not(inner))(lambda: pl.semaphore_wait(barrier, base + 1))


def remote(src, dst, send, recv, peer):
    return pltpu.make_async_remote_copy(
        src_ref=src, dst_ref=dst, send_sem=send, recv_sem=recv, device_id=peer, device_id_type=MESH
    )


def gather_body(count, lines, planes, in_ref, out_ref, local_sem, send, recv):
    y, x, c, z, to_x, to_y, to_p, dp = places()
    half = in_ref.shape[1] // 2
    low, high = pl.ds(0, half), pl.ds(half, half)
    greet(lines, planes, z, dp, (to_x, to_y, to_p))
    mine = out_ref.at[y, x, c] if planes else out_ref
    if lines:
        local = pltpu.make_async_copy(in_ref.at[0], mine.at[z], local_sem)
        steps = [(0, 1)] + [(j, side) for j in range(1, 4) for side in (-1, 1)]
    else:
        local = pltpu.make_async_copy(in_ref, mine, local_sem)
        steps = [(j, 1) for j in range(count)]
    local.start()

    def moved(kind, s, src, dst, peer):
        return remote(src, dst, send.at[kind, s], recv.at[kind, s], peer)

    def each(block):
        for j, side in steps:
            if lines and j:
                s = z + j * side
                pl.when((s >= 0) & (s <= 3))(functools.partial(block, s, j, side))
            else:
                block(z if lines else j, j, side)

    def along(s, side, src):
        return moved(0 if side < 0 else 10, s, src, mine.at[s], (dp, z - side))

    def x_of(s, src):
        return moved(1, s, src, mine.at[s], to_x)

    def y_of(s, src):
        return moved(2, s, src, mine.at[s], to_y)

    def p_of(s, src):
        return moved(3, s, src, mine.at[s], to_p)

    def first(s, j, side):
        src = in_ref.at[0 if lines else j] if not (lines and j) else mine.at[s]
        if lines:
            if j:
                along(s, side, src).wait_recv()
                pl.when((z - side >= 0) & (z - side <= 3))(lambda: along(s, side, src).start())
            else:
                pl.when(z < 3)(lambda: along(s, -1, src).start())
                pl.when(z > 0)(lambda: along(s, 1, src).start())
        if planes:
            x_of(s, src).start()
            y_of(s, src).start()
            p_of(s, src).start()

    def pair(s):
        one, two = out_ref.at[y, 1 - x, c, s], out_ref.at[1 - y, x, c, s]
        far = out_ref.at[1 - y, 1 - x, c, s]
        return (
            moved(4, s, one.at[low], one.at[low], to_y),
            moved(5, s, one, one, to_p),
            moved(6, s, two.at[high], two.at[high], to_x),
            moved(7, s, two, two, to_p),
            moved(8, s, far.at[low], far.at[low], to_p),
            moved(9, s, far.at[high], far.at[high], to_p),
        )

    def second(s, j, side):
        copies = pair(s)
        x_of(s, mine.at[s]).wait_recv()
        copies[0].start()
        copies[1].start()
        y_of(s, mine.at[s]).wait_recv()
        copies[2].start()
        copies[3].start()

    def third(s, j, side):
        copies = pair(s)
        copies[0].wait_recv()
        copies[4].start()
        copies[2].wait_recv()
        copies[5].start()

    def last(s, j, side):
        src = mine.at[s]
        if lines:
            if j:
                pl.when((z - side >= 0) & (z - side <= 3))(lambda: along(s, side, src).wait_send())
            else:
                pl.when(z < 3)(lambda: along(s, -1, src).wait_send())
                pl.when(z > 0)(lambda: along(s, 1, src).wait_send())
        if planes:
            copies = pair(s)
            p_of(s, src).wait_recv()
            for k in (1, 3, 4, 5):
                copies[k].wait_recv()
            for copy in (x_of(s, src), y_of(s, src), p_of(s, src)) + copies:
                copy.wait_send()

    each(first)
    if planes:
        each(second)
        each(third)
    each(last)
    local.wait()


def gather(own, lines, planes, identity):
    count = 4 if lines else own.shape[0]
    shape = ((2, 2, 2) if planes else ()) + (count,) + own.shape[1:]
    return pl.pallas_call(
        functools.partial(gather_body, count, lines, planes),
        out_shape=jax.ShapeDtypeStruct(shape, own.dtype),
        in_specs=[pl.BlockSpec(memory_space=pl.ANY)],
        out_specs=pl.BlockSpec(memory_space=pl.ANY),
        scratch_shapes=[
            pltpu.SemaphoreType.DMA,
            pltpu.SemaphoreType.DMA((11, count)),
            pltpu.SemaphoreType.DMA((11, count)),
        ],
        compiler_params=pltpu.CompilerParams(collective_id=identity, has_side_effects=True),
    )(own)


def add_rows(out, terms):
    rows = out.shape[0]
    step = 32 if rows % 32 == 0 else 16 if rows % 16 == 0 else 8

    def one(i, _):
        at = pl.ds(pl.multiple_of(i * step, step), step)
        total = terms[0][at].astype(F32)
        for term in terms[1:]:
            total = total + term[at].astype(F32)
        out[at] = total.astype(out.dtype)
        return 0

    lax.fori_loop(0, rows // step, one, 0)


def scatter_body(count, lines, in_ref, out_ref, *refs):
    own, from_p, from_y, from_x, whole_x, whole_y, *rest = refs
    from_z = rest.pop(0) if lines else None
    local_sem, send, recv = rest
    y, x, c, z, to_x, to_y, to_p, dp = places()
    half = out_ref.shape[-2] // 2
    low, high = pl.ds(0, half), pl.ds(half, half)
    z_peers = [(dp, (z + j) % 4) for j in range(1, 4)] if lines else []
    peers = z_peers + [to_x, to_y, to_p]
    barrier = pltpu.get_barrier_semaphore()
    for peer in peers:
        hello(peer)
    pl.semaphore_wait(barrier, len(peers))
    steps = [1, 2, 3, 0] if lines else list(range(count))
    order = [(z + j) % 4 if lines else j for j in steps]
    started = []

    def go(kind, j, src, dst, peer):
        copy = remote(src, dst, send.at[kind, j], recv.at[kind, j], peer)
        copy.start()
        started.append(copy)
        return copy

    firsts, seconds, thirds, along = [], [], [], []
    for j in range(count):
        other = go(1, j, in_ref.at[:, :, 1 - c, order[j]], from_p.at[j], to_p)
        local = pltpu.make_async_copy(in_ref.at[:, :, c, order[j]], own.at[j], local_sem.at[j])
        local.start()
        firsts.append((other, local))
    for j in range(count):
        firsts[j][1].wait()
        firsts[j][0].wait_recv()
        far = own.at[j, 1 - y, 1 - x]
        add_rows(far, [far, from_p.at[j, 1 - y, 1 - x]])
        seconds.append(
            (
                go(2, j, far.at[low], from_y.at[j], to_y),
                go(3, j, far.at[high], from_x.at[j], to_x),
            )
        )
        for yy, xx in ((y, 1 - x), (1 - y, x), (y, x)):
            add_rows(own.at[j, yy, xx], [own.at[j, yy, xx], from_p.at[j, yy, xx]])
    for j in range(count):
        seconds[j][0].wait_recv()
        side = own.at[j, y, 1 - x]
        add_rows(side.at[low], [side.at[low], from_y.at[j]])
        one = go(4, j, side, whole_x.at[j], to_x)
        seconds[j][1].wait_recv()
        side = own.at[j, 1 - y, x]
        add_rows(side.at[high], [side.at[high], from_x.at[j]])
        thirds.append((one, go(5, j, side, whole_y.at[j], to_y)))
    for j in range(count):
        thirds[j][0].wait_recv()
        thirds[j][1].wait_recv()
        mine = own.at[j, y, x]
        parts = [mine, whole_x.at[j], whole_y.at[j]]
        if not lines:
            add_rows(out_ref.at[j], parts)
        elif steps[j]:
            add_rows(mine, parts)
            at = steps[j] - 1
            along.append(go(0, steps[j], mine, from_z.at[at], z_peers[at]))
        else:
            for copy in along:
                copy.wait_recv()
            add_rows(out_ref, parts + [from_z.at[k] for k in range(3)])
    for copy in started:
        copy.wait_send()


def scatter_line_body(in_ref, out_ref, own, from_low, from_high, local_sem, send, recv):
    y, x, c, z, to_x, to_y, to_p, dp = places()
    greet(True, False, z, dp, ())
    local = pltpu.make_async_copy(in_ref, own, local_sem)
    local.start()

    def up(s):
        return remote(
            own.at[s], from_low.at[s], send.at[0, s], recv.at[0, s], (dp, z + 1)
        )

    def down(s):
        return remote(
            own.at[s], from_high.at[s], send.at[1, s], recv.at[1, s], (dp, z - 1)
        )

    def take(copy, s, arrived):
        copy(s).wait_recv()
        add_rows(own.at[s], [own.at[s], arrived.at[s]])

    def rising(s):
        pl.when(z > 0)(lambda: take(up, s, from_low))
        up(s).start()

    def falling(s):
        pl.when(z < 3)(lambda: take(down, s, from_high))
        down(s).start()

    local.wait()
    order = [jnp.where(z < 2, b, 3 - b) for b in (3, 0, 2, 1)]
    for s in order:
        pl.when(z < s)(functools.partial(rising, s))
        pl.when(z > s)(functools.partial(falling, s))
    pl.when(z > 0)(lambda: take(up, z, from_low))
    pl.when(z < 3)(lambda: take(down, z, from_high))
    add_rows(out_ref, [own.at[z]])
    for s in order:
        pl.when(z < s)(lambda s=s: up(s).wait_send())
        pl.when(z > s)(lambda s=s: down(s).wait_send())


def scatter_line(parts, identity):
    return pl.pallas_call(
        scatter_line_body,
        out_shape=jax.ShapeDtypeStruct(parts.shape[1:], parts.dtype),
        in_specs=[pl.BlockSpec(memory_space=pl.ANY)],
        out_specs=pl.BlockSpec(memory_space=pltpu.VMEM),
        scratch_shapes=[
            pltpu.VMEM(parts.shape, parts.dtype),
            pltpu.VMEM(parts.shape, parts.dtype),
            pltpu.VMEM(parts.shape, parts.dtype),
            pltpu.SemaphoreType.DMA,
            pltpu.SemaphoreType.DMA((2, 4)),
            pltpu.SemaphoreType.DMA((2, 4)),
        ],
        compiler_params=pltpu.CompilerParams(
            collective_id=identity, has_side_effects=True, vmem_limit_bytes=32 * 2**20
        ),
    )(parts)


def scatter(parts, lines, identity):
    count, rows, columns = parts.shape[-3:]
    buffer = lambda *lead: pltpu.VMEM(lead + (rows, columns), parts.dtype)
    halves = pltpu.VMEM((count, rows // 2, columns), parts.dtype)
    scratch = [buffer(count, 2, 2), buffer(count, 2, 2), halves, halves, buffer(count), buffer(count)]
    if lines:
        scratch.append(buffer(3))
    scratch += [
        pltpu.SemaphoreType.DMA((count,)),
        pltpu.SemaphoreType.DMA((6, count)),
        pltpu.SemaphoreType.DMA((6, count)),
    ]
    return pl.pallas_call(
        functools.partial(scatter_body, count, lines),
        out_shape=jax.ShapeDtypeStruct(
            (rows, columns) if lines else (count, rows, columns), parts.dtype
        ),
        in_specs=[pl.BlockSpec(memory_space=pl.ANY)],
        out_specs=pl.BlockSpec(memory_space=pltpu.VMEM),
        scratch_shapes=scratch,
        compiler_params=pltpu.CompilerParams(
            collective_id=identity, has_side_effects=True, vmem_limit_bytes=48 * 2**20
        ),
    )(parts)


PIECES = 4


class Moves:
    def __init__(self, ND, NF):
        self.ND, self.NF = ND, NF
        self.fast = (ND, NF) == (8, 4)

    def gather_dp(self, rows, identity):
        if not self.fast:
            return lax.all_gather(rows, "dp", axis=0, tiled=True)
        T, C = rows.shape
        return gather(rows.reshape(PIECES, T // PIECES, C), False, True, identity).reshape(
            self.ND * T, C
        )

    def gather_fsdp(self, rows, identity):
        if not self.fast:
            return lax.all_gather(rows, "fsdp", axis=0, tiled=False)
        return gather(rows[None], True, False, identity)

    def gather_all(self, rows, identity):
        if not self.fast:
            return lax.all_gather(rows, BOTH, axis=0, tiled=False)
        return gather(rows[None], True, True, identity).reshape((-1,) + rows.shape)

    def scatter_dp(self, parts, identity):
        if not self.fast:
            return lax.psum_scatter(parts, "dp", scatter_dimension=0, tiled=True)
        T, C = parts.shape[0] // self.ND, parts.shape[1]
        return scatter(
            parts.reshape(2, 2, 2, PIECES, T // PIECES, C), False, identity
        ).reshape(T, C)

    def scatter_fsdp(self, parts, identity):
        if not self.fast:
            return lax.psum_scatter(parts, "fsdp", scatter_dimension=0, tiled=False)
        return scatter_line(parts, identity)

    def scatter_all(self, parts, identity):
        count, R, C = parts.shape
        if not self.fast:
            return lax.psum_scatter(
                parts.reshape(count * R, C), BOTH, scatter_dimension=0, tiled=True
            )
        return scatter(parts.reshape(2, 2, 2, self.NF, R, C), True, identity)


def pack(pieces):
    packed = jnp.concatenate([piece.reshape(-1, LANES) for piece in pieces], axis=0)
    return jnp.pad(packed, ((0, -packed.shape[0] % 16), (0, 0)))


def unpack(full, pieces):
    out, at = [], 0
    for piece in pieces:
        size = piece.size // LANES
        part = full[:, at : at + size]
        out.append(part.reshape(full.shape[0] * piece.shape[0], piece.shape[1]))
        at += size
    return lax.optimization_barrier(tuple(out))


def pack_grads(grads, count):
    packed = jnp.concatenate([g.astype(BF16).reshape(count, -1, LANES) for g in grads], axis=1)
    return jnp.pad(packed, ((0, 0), (0, -packed.shape[1] % 64), (0, 0)))


def unpack_grads(summed, grads, count):
    out, at = [], 0
    for g in grads:
        size = g.size // count // LANES
        out.append(summed[at : at + size].reshape(g.shape[0] // count, g.shape[1]).astype(F32))
        at += size
    return out


def per_device_of(ND, NF):
    COUNT = ND * NF
    moves = Moves(ND, NF)

    def per_device(
        layer_input,
        output_gradient,
        prefix_length,
        attention_gain,
        inward,
        inward_down,
        inward_up,
        outward,
        outward_down,
        outward_up,
        feedforward_gain,
        widening,
        widening_down,
        widening_up,
        narrowing,
        narrowing_down,
        narrowing_up,
    ):
        micro_count, _, T, D = layer_input.shape
        QKV = inward.shape[1]
        query_width = outward.shape[0] * COUNT
        HEADS = query_width // HDIM
        FF = widening.shape[1] // 2
        RANK = widening_down.shape[1]
        FS = FF // ND
        FP = -(-FS // LANES) * LANES
        ROWS = D // COUNT
        UPS = RANK // COUNT
        scale = HDIM ** (-0.5)

        gains = jnp.pad(
            jnp.stack([attention_gain, feedforward_gain]), ((0, 0), (0, LANES - ROWS))
        )
        pieces = (
            gains,
            inward,
            inward_down,
            inward_up,
            outward,
            outward_down,
            outward_up,
            widening_down,
            narrowing_up,
        )
        (
            gains_full,
            inward_full,
            inward_down_full,
            inward_up_full,
            outward_full,
            outward_down_full,
            outward_up_full,
            widening_down_full,
            narrowing_up_full,
        ) = unpack(moves.gather_all(pack(pieces), 1), pieces)
        gains_full = gains_full.reshape(COUNT, 2, LANES)[:, :, :ROWS].astype(F32)
        first_gain = gains_full[:, 0].reshape(D)
        second_gain = gains_full[:, 1].reshape(D)
        wide = jnp.concatenate([widening, widening_up], axis=0)
        wide = wide.reshape(ROWS + UPS, 2, ND, FS)
        wide = jnp.pad(wide, ((0, 0), (0, 0), (0, 0), (0, FP - FS)))
        wide = wide.transpose(2, 0, 1, 3).reshape(ND, ROWS + UPS, 2 * FP)
        wide = lax.all_to_all(wide, "dp", 0, 0, tiled=True)
        wide = lax.all_gather(wide, "fsdp", axis=0, tiled=False)
        wide = wide.transpose(1, 0, 2, 3)
        widening_slice = wide[:, :, :ROWS].reshape(D, 2 * FP)
        widening_up_slice = wide[:, :, ROWS:].reshape(RANK, 2 * FP)
        narrow = jnp.concatenate([narrowing, narrowing_down], axis=1)
        narrow = lax.all_gather(narrow, "fsdp", axis=0, tiled=True)
        narrow = jnp.pad(narrow, ((0, FP - FS), (0, 0)))
        narrowing_slice, narrowing_down_slice = narrow[:, :D], narrow[:, D:]

        inward_eff = (inward_full + product(inward_down_full, inward_up_full)).astype(BF16)
        outward_eff = (outward_full + product(outward_down_full, outward_up_full)).astype(BF16)
        wide_eff = (widening_slice + product(widening_down_full, widening_up_slice)).astype(BF16)
        narrow_eff = (narrowing_slice + product(narrowing_down_slice, narrowing_up_full)).astype(
            BF16
        )

        positions = lax.axis_index("fsdp") * T + jnp.arange(T, dtype=jnp.int32)
        cosine, sine_part = rotation(positions, HDIM)

        def unit(v):
            return v * lax.rsqrt(jnp.mean(v * v, axis=-1, keepdims=True) + EPSILON)

        def unit_back(v, gain, upstream):
            r = lax.rsqrt(jnp.mean(v * v, axis=-1, keepdims=True) + EPSILON)
            n = v * r
            e = upstream * gain
            back = r * (e - n * jnp.mean(e * n, axis=-1, keepdims=True))
            return back, jnp.sum(upstream * n, axis=0)

        M = micro_count
        R = M * T
        per_micro = lambda a: a.reshape((M, T) + a.shape[1:])
        cosine_all = jnp.concatenate([cosine] * M, axis=0)
        sine_all = jnp.concatenate([sine_part] * M, axis=0)
        head_cosine, head_sine = cosine_all[:, None, :], sine_all[:, None, :]

        residual = layer_input.reshape(R, D).astype(F32)
        upstream = output_gradient.reshape(R, D)
        upstream_all = lax.all_gather(upstream, "dp", axis=0, tiled=True)

        normed_first = (unit(residual) * first_gain).astype(BF16)
        joint = product(normed_first, inward_eff)
        queries = rotate(
            joint[:, :query_width].reshape(R, HEADS, HDIM), head_cosine, head_sine
        ).astype(BF16)
        queries = per_micro(queries)
        own_keys = rotate(joint[:, query_width : query_width + HDIM], cosine_all, sine_all)
        own = jnp.concatenate([own_keys, joint[:, query_width + HDIM :]], axis=1).astype(BF16)
        both = moves.gather_fsdp(own, 3).reshape(NF, M, T, 2 * HDIM)
        both = both.transpose(1, 0, 2, 3).reshape(M, NF * T, 2 * HDIM)
        all_keys, all_values = both[..., :HDIM], both[..., HDIM:]
        key_pos = jnp.arange(NF * T, dtype=jnp.int32)
        visible = (key_pos[None, None, :] <= positions[None, :, None]) | (
            key_pos[None, None, :] < prefix_length[:, :, None]
        )

        def masked_scores():
            raw = (
                jnp.einsum("mrhd,mkd->mhrk", queries, all_keys, preferred_element_type=F32) * scale
            )
            return jnp.where(visible[:, None], raw, -1e30)

        scores = masked_scores()
        peak = jnp.max(scores, axis=-1, keepdims=True)
        logsum = peak + jnp.log(jnp.sum(jnp.exp(scores - peak), axis=-1, keepdims=True))
        probs_low = jnp.exp(scores - logsum).astype(BF16)
        mix = jnp.einsum("mhrk,mkd->mrhd", probs_low, all_values, preferred_element_type=F32)
        mixed = mix.reshape(R, query_width).astype(BF16)
        middle = residual + product(mixed, outward_eff)
        normed_second = (unit(middle) * second_gain).astype(BF16)
        second_all = moves.gather_dp(normed_second, 4)

        spread = product(second_all, wide_eff)
        gate, upper = spread[:, :FP], spread[:, FP:]
        value, slope = gelu_parts(gate)
        activated = (value * upper).astype(BF16)
        shrink = product(activated, narrow_eff).astype(BF16)
        shrink = lax.psum_scatter(shrink, "dp", scatter_dimension=0, tiled=True)
        outputs = (middle + shrink.astype(F32)).astype(BF16)
        narrow_grad = contract_rows(activated, upstream_all).astype(BF16)
        act_grad = against(upstream_all, narrow_eff)
        spread_grad = jnp.concatenate(
            [act_grad * upper * slope, act_grad * value], axis=1
        ).astype(BF16)
        wide_grad = contract_rows(second_all, spread_grad).astype(BF16)
        rows_grad = against(spread_grad, wide_eff).astype(BF16)
        rows_grad = moves.scatter_dp(rows_grad, 5)
        back, second_gain_grad = unit_back(middle, second_gain, rows_grad.astype(F32))
        middle_grad = upstream.astype(F32) + back
        branch_grad = middle_grad.astype(BF16)

        wide_up_grad = contract_rows(widening_down_full, wide_grad).astype(BF16)
        widening_down_part = against(wide_grad, widening_up_slice)
        narrowing_up_part = contract_rows(narrowing_down_slice, narrow_grad)
        wide_both = jnp.concatenate(
            [
                wide_grad.reshape(ND, NF, ROWS, 2 * FP),
                wide_up_grad.reshape(ND, NF, UPS, 2 * FP),
            ],
            axis=2,
        ).transpose(1, 0, 2, 3)
        wide_both = wide_both.reshape(NF * ND * (ROWS + UPS), 2 * FP)
        wide_both = lax.psum_scatter(wide_both, "fsdp", scatter_dimension=0, tiled=True)
        wide_both = wide_both.reshape(ND, ROWS + UPS, 2 * FP)
        wide_both = lax.all_to_all(wide_both, "dp", 0, 0, tiled=True)
        wide_both = wide_both.reshape(ND, ROWS + UPS, 2, FP)[..., :FS].transpose(1, 2, 0, 3)
        wide_both = wide_both.reshape(ROWS + UPS, 2 * FF).astype(F32)
        widening_grad, widening_up_grad = wide_both[:ROWS], wide_both[ROWS:]
        narrow_sum = lax.psum_scatter(narrow_grad[:FS], "fsdp", scatter_dimension=0, tiled=True)
        narrowing_grad = narrow_sum.astype(F32)
        narrowing_down_grad = against(narrow_sum, narrowing_up_full)

        mixed_grad = against(branch_grad, outward_eff).astype(BF16)
        mixed_grad = mixed_grad.reshape(M, T, HEADS, HDIM)
        probs_again = jnp.exp(masked_scores() - logsum)
        prob_grad = jnp.einsum(
            "mrhd,mkd->mhrk", mixed_grad, all_values, preferred_element_type=F32
        )
        center = jnp.sum(probs_again * prob_grad, axis=-1, keepdims=True)
        score_grad = (probs_again * (prob_grad - center)).astype(BF16)
        key_grad = (
            jnp.einsum("mhrk,mrhd->mkd", score_grad, queries, preferred_element_type=F32) * scale
        )
        value_grad = jnp.einsum(
            "mhrk,mrhd->mkd", probs_again.astype(BF16), mixed_grad, preferred_element_type=F32
        )
        both = jnp.concatenate([key_grad, value_grad], axis=-1).astype(BF16)
        both = both.reshape(M, NF, T, 2 * HDIM).transpose(1, 0, 2, 3).reshape(NF, R, 2 * HDIM)
        both = moves.scatter_fsdp(both, 7).astype(F32)
        query_grad = (
            jnp.einsum("mhrk,mkd->mrhd", score_grad, all_keys, preferred_element_type=F32) * scale
        ).reshape(R, HEADS, HDIM)
        joint_grad = jnp.concatenate(
            [
                rotate(query_grad, head_cosine, -head_sine).reshape(R, query_width),
                rotate(both[:, :HDIM], cosine_all, -sine_all),
                both[:, HDIM:],
            ],
            axis=1,
        ).astype(BF16)
        first_rows_grad = against(joint_grad, inward_eff)
        back, first_gain_grad = unit_back(residual, first_gain, first_rows_grad)
        input_grads = middle_grad + back

        outward_part = contract_rows(mixed, branch_grad).astype(BF16)
        outward_up_part = contract_rows(outward_down_full, outward_part)
        inward_part = contract_rows(normed_first, joint_grad).astype(BF16)
        inward_up_part = contract_rows(inward_down_full, inward_part)
        gain_parts = jnp.stack([first_gain_grad, second_gain_grad]).reshape(2, COUNT, ROWS)
        gain_parts = jnp.pad(gain_parts, ((0, 0), (0, 0), (0, LANES - ROWS)))
        gain_parts = gain_parts.transpose(1, 0, 2).reshape(COUNT * 2, LANES)
        parts = (
            outward_part,
            outward_up_part,
            widening_down_part,
            narrowing_up_part,
            inward_part,
            inward_up_part,
            gain_parts,
        )
        (
            outward_grad,
            outward_up_grad,
            widening_down_grad,
            narrowing_up_grad,
            inward_grad,
            inward_up_grad,
            gain_grads,
        ) = unpack_grads(moves.scatter_all(pack_grads(parts, COUNT), 6), parts, COUNT)
        outward_down_grad = against(outward_grad.astype(BF16), outward_up_full)
        inward_down_grad = against(inward_grad.astype(BF16), inward_up_full)

        return (
            outputs.reshape(layer_input.shape),
            input_grads.reshape(layer_input.shape),
            gain_grads[0, :ROWS],
            inward_grad,
            inward_down_grad,
            inward_up_grad,
            outward_grad,
            outward_down_grad,
            outward_up_grad,
            gain_grads[1, :ROWS],
            widening_grad,
            widening_down_grad,
            widening_up_grad,
            narrowing_grad,
            narrowing_down_grad,
            narrowing_up_grad,
        )

    return per_device


def solution(mesh):
    rows = P(BOTH, None)
    tokens = P(None, "dp", "fsdp", None)
    weights = (P(BOTH),) + (rows,) * 6 + (P(BOTH),) + (rows,) * 6
    return jax.shard_map(
        per_device_of(mesh.shape["dp"], mesh.shape["fsdp"]),
        mesh=mesh,
        in_specs=(tokens, tokens, P(None, "dp")) + weights,
        out_specs=(tokens, tokens) + weights,
        check_vma=False,
    )
```
